32 devices in a mesh: slices: 2 (over y), modes: 4 (over z), half: 4 (over x, core).
Axes of the slice: x: 2, y: 2, z: 4, core: 2. Of those that a mesh axis runs over, the one named last changes fastest.
Arguments:
- stem_state: bfloat16 [2, 8, 4, 2, 128, 128], P(None, ('slices', 'modes'), 'half'), parts along dimension 1, may hold values from -6 to 6
- branch_mats: bfloat16 [4, 6, 2, 128, 128], replicated, may hold values from -1 to 1
- branch_modes: int32 [4, 6], replicated, may hold values from 0 to 1
- out_proj: bfloat16 [4, 2, 512, 256], P('half'), may hold values from -0.1875 to 0.1875
- groups: int32 [8, 4, 64, 1], P(('slices', 'modes'), 'half'), parts along dimension 0, may hold values from 0 to 3; in each aligned block of 64 rows (0 to 63, 64 to 127, ..., all dimensions but the last counted through in order) at most 16 rows name the same one
Outputs:
- amplitudes: bfloat16 [8, 4, 2, 64, 256], P(('slices', 'modes'), 'half'), parts along dimension 0
The draws below stay inside these ranges and needn't reach their ends.
There are 2 independent parts, one for each index of `slices`. The reference program is written for one: setup_inputs(seed, part) draws one part's arguments, and reference() takes and returns one part's arrays. A program takes and returns all parts, laid end to end along the dimension named above; an argument that names none is the same for every part. Nothing has to cross between parts.
Inputs may be any that keep to these rules, and one draw needn't show every extreme that they name: `branch_modes`: 0: the branch contracts the fifth index b of the state, 1: the sixth index c. `groups`: the 64 rows of one device name one group at most 16 times, and some device names some group exactly 16 times.
All inputs are finite; a program needn't handle non-finite values.
Results may differ from the reference program's by a relative error of at most 0.025.
Values may be sent and summed in bfloat16 or wider, within the bound.
No kernel may reach another device: no remote copies, remote signals or barrier semaphores. Data moves between devices by JAX's collectives and lax.ppermute only.
A program may use at most 64 MiB of HBM per device.

```python
import math
import jax
import jax.numpy as jnp
import numpy as np
from jax import lax

BRANCH = 128
STEM = 512
OUT_WIDTH = 256
LEGS = 4
BRANCHES = 6
SLABS = 2
ROWS_DEV = 64
CAPACITY = 16
N_MODES = 4
N_HALF = 4


def draw_branch_mats(key, part):
    base = jax.random.fold_in(key, 7)
    key_angle = jax.random.fold_in(base, 1)
    key_real = jax.random.fold_in(base, 2)
    key_imag = jax.random.fold_in(base, 3)
    angles = jax.random.uniform(key_angle, (LEGS, BRANCHES, BRANCH), jnp.float32, -math.pi, math.pi)
    sigma = 0.25 / math.sqrt(2.0 * BRANCH)
    shape = (LEGS, BRANCHES, BRANCH, BRANCH)
    noise_real = jax.random.normal(key_real, shape, jnp.float32) * sigma
    noise_imag = jax.random.normal(key_imag, shape, jnp.float32) * sigma
    identity = jnp.eye(BRANCH, dtype=jnp.float32)
    offdiag = 1.0 - identity
    diag_real = identity * jnp.cos(angles)[..., :, None]
    diag_imag = identity * jnp.sin(angles)[..., :, None]
    factor = 1.0 / math.sqrt(1.0625)
    real_part = (diag_real + noise_real * offdiag) * factor
    imag_part = (diag_imag + noise_imag * offdiag) * factor
    stacked = jnp.stack([real_part, imag_part], axis=2)
    return jnp.clip(stacked, -1.0, 1.0).astype(jnp.bfloat16)


def touch_ends(drawn, stream_key, low, high):
    place = [jax.random.randint(jax.random.fold_in(stream_key, axis), (), 0, length) for axis, length in enumerate(drawn.shape)]
    main_axis = drawn.shape.index(max(drawn.shape))
    next_to = place[:main_axis] + [(place[main_axis] + 1) % drawn.shape[main_axis]] + place[main_axis + 1:]
    return drawn.at[tuple(place)].set(low).at[tuple(next_to)].set(high)


def block_scale(stream_key, shape, split, smallest, top_value):
    gain, own = 1.0, jax.random.fold_in(stream_key, 6)
    for position, parts in split:
        heights = jnp.exp(jax.random.uniform(jax.random.fold_in(own, position), (parts,), jnp.float32, smallest / len(split), top_value / len(split)))
        gain = gain * jnp.repeat(heights, shape[position] // parts).reshape([-1 if axis == position else 1 for axis in range(len(shape))])
    return gain


def shared_out(own_key, own, number, rows, count, top, reach, skew):
    order = jax.random.permutation(own_key, count)
    crowded, common = load_shares(count, rows * top, reach, skew, True), load_shares(count, rows * top, reach, skew, False)
    places = jnp.arange(count)

    def named(lengths, rotation):
        used = int((lengths > 0).sum())
        fixed = max(1, used // 4)
        moved = fixed + (places - fixed + rotation * (used - fixed)) % max(1, count - fixed)
        return jnp.zeros((count,), jnp.int32).at[order[jnp.where(places < fixed, places, moved)]].set(jnp.asarray(lengths, jnp.int32))

    lengths = jnp.where(number % 4 == 0, named(crowded, number // 4), named(common, number - number // 4 - 1))
    mixed = jax.random.permutation(jax.random.fold_in(own, 3), count)
    giver, taker = mixed[0:count // 2 * 2:2], mixed[1:count // 2 * 2:2]
    slack = jnp.minimum(lengths[giver] - 1, reach - lengths[taker]) // 2
    slack = jnp.where((giver == order[0]) | (taker == order[0]) | (lengths[taker] == 0), 0, jnp.maximum(slack, 0))
    moved = jax.random.randint(jax.random.fold_in(own, 4), (count // 2,), 0, 1 << 20) % (slack + 1)
    lengths = lengths.at[giver].add(-moved).at[taker].add(moved)
    members = jnp.searchsorted(jnp.cumsum(lengths), jnp.arange(rows * top), side="right").astype(jnp.int32)
    table = members.reshape(top, rows).T
    table = table[jax.random.permutation(jax.random.fold_in(own, 1), rows)]
    rotation = jax.random.randint(jax.random.fold_in(own, 2), (rows, 1), 0, top)
    return jnp.take_along_axis(table, (jnp.arange(top)[None, :] + rotation) % top, axis=1)


def load_shares(amount, total, limit, slope, full):
    weights = [(1 << 20) // math.isqrt(grade ** slope) + 1 for grade in range(1, amount + 1)]
    largest = limit if full else min(limit, max(-(-total // amount), total * weights[0] // sum(weights)))
    least = 1 if total - largest >= amount - 1 else 0
    given, spare = [largest] + [least] * (amount - 1), total - largest - least * (amount - 1)
    while spare > 0:
        candidates = [i for i in range(1, amount) if given[i] < largest] or [i for i in range(1, amount) if given[i] < limit]
        pool, left = sum([weights[i] for i in candidates]), spare
        for i in candidates:
            extra = min(limit - given[i], max(1, left * weights[i] // pool), spare)
            given[i] = given[i] + extra
            spare = spare - extra
    return np.array(given)


def normal_values(stream_key, extent, width, limit, split=(), kind=jnp.bfloat16):
    gain = block_scale(stream_key, extent, split, -0.22, 0.18) if split else 1.0
    drawn = jax.random.normal(stream_key, extent, jnp.float32) * width * gain
    return jnp.minimum(jnp.maximum(drawn, -limit), limit).astype(kind)


def setup_inputs(seed: int = 0, part: int = 0) -> dict:
    keys = jax.random.split(jax.random.key(seed), 6)
    part_splits = jax.random.split(jax.random.fold_in(keys[5], part), 6)
    stem_state = normal_values(part_splits[0], (2, N_MODES, N_HALF, SLABS, BRANCH, BRANCH), 1.0, 6.0, ((1, 4), (2, 4)))
    branch_mats = draw_branch_mats(jax.random.fold_in(keys[5], 71), part)
    branch_modes = touch_ends(jax.random.randint(keys[2], (LEGS, BRANCHES), 0, 2), jax.random.fold_in(keys[2], 1), 0, 1).astype(jnp.int32)
    out_proj = normal_values(keys[3], (N_HALF, 2, STEM, OUT_WIDTH), (2 * STEM) ** -0.5, 0.1875, ((0, 4),))
    groups_keys = jax.random.split(jax.random.fold_in(part_splits[4], 1), N_MODES * N_HALF * ROWS_DEV // ROWS_DEV)
    groups_turns = jax.random.permutation(jax.random.fold_in(part_splits[4], 3), N_MODES * N_HALF * ROWS_DEV // ROWS_DEV)
    groups = jax.vmap(lambda own, number: shared_out(jax.random.fold_in(part_splits[4], 2), own, number, ROWS_DEV, N_HALF, 1, CAPACITY, 2))(groups_keys, groups_turns).reshape((N_MODES, N_HALF, ROWS_DEV, 1))
    return dict(stem_state=stem_state, branch_mats=branch_mats, branch_modes=branch_modes, out_proj=out_proj, groups=groups)


def widen(matrix):
    real_part = matrix[0]
    imag_part = matrix[1]
    return jnp.stack([jnp.stack([real_part, imag_part]), jnp.stack([-imag_part, real_part])])


def contract_first(state, wide):
    value = jnp.einsum('imhsbc,ijbd->jmhsdc', state.astype(jnp.float32), wide.astype(jnp.float32), precision=lax.Precision.HIGHEST)
    return value.astype(jnp.bfloat16)


def contract_second(state, wide):
    value = jnp.einsum('imhsbc,ijcd->jmhsbd', state.astype(jnp.float32), wide.astype(jnp.float32), precision=lax.Precision.HIGHEST)
    return value.astype(jnp.bfloat16)


def swap_modes(state):
    comps, nmodes, nhalf, slabs, inner, outer = state.shape
    spread = state.reshape(comps, nmodes, nhalf, slabs, inner, nmodes, outer // nmodes)
    spread = jnp.swapaxes(spread, 1, 5)
    return spread.reshape(comps, nmodes, nhalf, slabs, inner, outer)


def reference(stem_state, branch_mats, branch_modes, out_proj, groups):
    state = stem_state
    for leg in range(LEGS):
        for branch in range(BRANCHES):
            wide = widen(branch_mats[leg, branch])
            state = lax.cond(branch_modes[leg, branch] == 0, contract_first, contract_second, state, wide)
        state = swap_modes(state)
    comps, nmodes, nhalf = state.shape[0], state.shape[1], state.shape[2]
    rows = state.reshape(comps, nmodes, nhalf, ROWS_DEV, STEM).astype(jnp.float32)
    chosen = groups[..., 0]
    result = jnp.zeros((2, nmodes, nhalf, ROWS_DEV, OUT_WIDTH), jnp.float32)
    for owner in range(N_HALF):
        wide = widen(out_proj[owner]).astype(jnp.float32)
        product = jnp.einsum('imhrk,ijkd->jmhrd', rows, wide, precision=lax.Precision.HIGHEST)
        result = jnp.where((chosen == owner)[None, :, :, :, None], product, result)
    return jnp.transpose(result, (1, 2, 0, 3, 4)).astype(jnp.bfloat16)
```

```python
import functools

import jax
import jax.numpy as jnp
from jax import lax
from jax.experimental import pallas as pl
from jax.experimental.pallas import tpu as pltpu
from jax.sharding import PartitionSpec as P


BF16 = jnp.bfloat16
F32 = jnp.float32


def chain_kernel(peers, modes_ref, mats_ref, w_ref, a_ref, t_ref, u_ref):
    legs, branches, _, n, _ = mats_ref.shape
    part = n // peers
    me = lax.axis_index("modes")
    row = lax.broadcasted_iota(jnp.int32, (n, n), 0)
    col = lax.broadcasted_iota(jnp.int32, (n, n), 1)
    for m in range(peers):
        hit = (col // part == m) & (row == me * part + col % part)
        t_ref[0:n, m * n : (m + 1) * n] = hit.astype(F32).astype(BF16)
    t_ref[n : 2 * n, :] = jnp.zeros((n, peers * n), BF16)
    u_ref[0:n, :] = (row == col).astype(F32).astype(BF16)
    u_ref[n : 2 * n, :] = jnp.zeros((n, n), BF16)

    def swap():
        old = t_ref[...]
        for half in range(2):
            for m in range(peers):
                for t in range(peers):
                    if m != t:
                        t_ref[
                            half * n + t * part : half * n + (t + 1) * part, m * n : (m + 1) * n
                        ] = old[
                            half * n + m * part : half * n + (m + 1) * part, t * n : (t + 1) * n
                        ]

    for step in range(legs):
        leg = legs - 1 - step

        def branch(i, carry):
            j = branches - 1 - i
            real = mats_ref[leg, j, 0]
            imag = mats_ref[leg, j, 1]
            wide = jnp.concatenate(
                [jnp.concatenate([real, -imag], axis=1), jnp.concatenate([imag, real], axis=1)],
                axis=0,
            )

            @pl.when(modes_ref[leg, j] == 0)
            def _():
                u_ref[...] = jnp.dot(wide, u_ref[...], preferred_element_type=F32).astype(BF16)

            @pl.when(modes_ref[leg, j] != 0)
            def _():
                t_ref[...] = jnp.dot(wide, t_ref[...], preferred_element_type=F32).astype(BF16)

            return carry

        lax.fori_loop(0, branches, branch, 0)
        if step < legs - 1:
            swap()

    for m in range(peers):
        real = t_ref[0:n, m * n : (m + 1) * n]
        imag = t_ref[n : 2 * n, m * n : (m + 1) * n]
        w_ref[m, 0:n, 0:n] = real
        w_ref[m, 0:n, n : 2 * n] = imag
        w_ref[m, n : 2 * n, 0:n] = -imag
        w_ref[m, n : 2 * n, n : 2 * n] = real
    fold = a_ref.shape[0] // 2 // 32
    pick = (col == fold * (row % 32) + row // 32).astype(F32).astype(BF16)
    turn = functools.partial(
        lax.dot_general, dimension_numbers=(((1,), (1,)), ((), ())), preferred_element_type=F32
    )
    real = turn(pick, u_ref[0:n, :]).astype(BF16)
    imag = turn(pick, u_ref[n : 2 * n, :]).astype(BF16)
    a_ref[0:n, 0:n] = real
    a_ref[0:n, n : 2 * n] = -imag
    a_ref[n : 2 * n, 0:n] = imag
    a_ref[n : 2 * n, n : 2 * n] = real


def stem_kernel(peers, owners, fold, chosen_ref, w_ref, a_ref, *refs):
    states = refs[:peers]
    projs = refs[peers : peers + owners]
    out_ref = refs[peers + owners]
    me = lax.axis_index("modes")
    mine = lax.axis_index("half")
    n = a_ref.shape[0] // 2
    slabs = states[0].shape[1]
    total = None
    for slot in range(peers):
        state = states[slot]
        flat = [state[part].reshape(slabs * n, n) for part in range(2)]
        term = jnp.dot(
            jnp.concatenate(flat, axis=1), w_ref[me ^ slot], preferred_element_type=F32
        )
        total = term if total is None else total + term
    total = total.astype(BF16)
    sides = [
        jnp.concatenate(
            [total[s * n : (s + 1) * n, part * n : (part + 1) * n] for s in range(slabs)], axis=1
        )
        for part in range(2)
    ]
    turned = jnp.dot(
        a_ref[...], jnp.concatenate(sides, axis=0), preferred_element_type=F32
    ).astype(BF16)
    span = n // fold
    rows = jnp.concatenate(
        [
            jnp.concatenate(
                [
                    turned[part * n + q * span : part * n + (q + 1) * span, s * n : (s + 1) * n]
                    for q in range(fold)
                ],
                axis=1,
            )
            for part in range(2)
            for s in range(slabs)
        ],
        axis=0,
    )
    count = slabs * span
    chosen = chosen_ref[...]
    chosen = jnp.concatenate([chosen, chosen], axis=0)
    out_real = None
    for slot in range(owners):
        kept = jnp.where(chosen == (mine ^ slot), rows, jnp.zeros_like(rows))
        with_real = jnp.dot(kept, projs[slot][0], preferred_element_type=F32)
        with_imag = jnp.dot(kept, projs[slot][1], preferred_element_type=F32)
        real = with_real[:count] - with_imag[count:]
        imag = with_imag[:count] + with_real[count:]
        out_real = real if out_real is None else out_real + real
        out_imag = imag if slot == 0 else out_imag + imag
    out_ref[0] = out_real.astype(BF16)
    out_ref[1] = out_imag.astype(BF16)


def pair(value, axis, distance):
    size = lax.axis_size(axis)
    return lax.ppermute(value, axis, [(i, i ^ distance) for i in range(size)])


def vmem(count):
    return [pl.BlockSpec(memory_space=pltpu.VMEM)] * count


def gathered(stem_state, branch_mats, branch_modes, out_proj, groups):
    peers = lax.axis_size("modes")
    owners = lax.axis_size("half")
    slabs, n = stem_state.shape[3], stem_state.shape[4]
    stem_len, out_len = out_proj.shape[2], out_proj.shape[3]
    row_total = slabs * n * n // stem_len
    fold = stem_len // n
    state = stem_state.reshape(2, slabs, n, n)
    proj = out_proj.reshape(2, stem_len, out_len)
    far = pair(proj, "half", 2)
    near = pair(proj, "half", 1)
    states = [state] + [pair(state, "modes", d) for d in range(1, peers)]
    w, a = pl.pallas_call(
        functools.partial(chain_kernel, peers),
        out_shape=(
            jax.ShapeDtypeStruct((peers, 2 * n, 2 * n), BF16),
            jax.ShapeDtypeStruct((2 * n, 2 * n), BF16),
        ),
        in_specs=[pl.BlockSpec(memory_space=pltpu.SMEM)] + vmem(1),
        out_specs=tuple(vmem(2)),
        scratch_shapes=[pltpu.VMEM((2 * n, peers * n), BF16), pltpu.VMEM((2 * n, n), BF16)],
        cost_estimate=pl.CostEstimate(
            flops=4_000_000_000, bytes_accessed=8_000_000, transcendentals=0
        ),
        compiler_params=pltpu.CompilerParams(vmem_limit_bytes=12 << 20),
        name="chain",
    )(branch_modes, branch_mats)
    far, w = lax.optimization_barrier((far, w))
    far_near = pair(far, "half", 1)
    projs = [proj, near, far, far_near]
    out = pl.pallas_call(
        functools.partial(stem_kernel, peers, owners, fold),
        out_shape=jax.ShapeDtypeStruct((2, row_total, out_len), BF16),
        in_specs=vmem(3 + peers + owners),
        out_specs=vmem(1)[0],
        compiler_params=pltpu.CompilerParams(vmem_limit_bytes=16 << 20),
        name="stem",
    )(groups.reshape(row_total, 1), w, a, *states, *projs)
    return out.reshape(1, 1, 2, row_total, out_len)


def widen(matrix):
    real_part = matrix[0]
    imag_part = matrix[1]
    return jnp.stack([jnp.stack([real_part, imag_part]), jnp.stack([-imag_part, real_part])])


def contract_first(state, wide):
    value = jnp.einsum("isbc,ijbd->jsdc", state, wide, preferred_element_type=jnp.float32)
    return value.astype(jnp.bfloat16)


def contract_second(state, wide):
    value = jnp.einsum("isbc,ijcd->jsbd", state, wide, preferred_element_type=jnp.float32)
    return value.astype(jnp.bfloat16)


def stepped(stem_state, branch_mats, branch_modes, out_proj, groups):
    slabs = stem_state.shape[3]
    inner = stem_state.shape[4]
    state = stem_state.reshape(2, slabs, inner, inner)
    legs_total = branch_mats.shape[0]
    branch_total = branch_mats.shape[1]
    peers = lax.axis_size("modes")
    width_part = inner // peers
    for leg in range(legs_total):

        def advance(branch, current):
            wide = widen(branch_mats[leg][branch])
            return lax.cond(
                branch_modes[leg][branch] == 0, contract_first, contract_second, current, wide
            )

        state = lax.fori_loop(0, branch_total, advance, state)
        pieces = state.reshape(2, slabs, inner, peers, width_part)
        pieces = jnp.transpose(pieces, (3, 0, 1, 2, 4)).reshape(peers, 2, slabs, inner * width_part)
        pieces = lax.all_to_all(pieces, "modes", split_axis=0, concat_axis=0, tiled=True)
        pieces = pieces.reshape(peers, 2, slabs, inner, width_part)
        state = jnp.transpose(pieces, (1, 2, 3, 0, 4)).reshape(2, slabs, inner, inner)
    stem_len = out_proj.shape[2]
    out_len = out_proj.shape[3]
    row_total = slabs * inner * inner // stem_len
    rows = state.reshape(2, row_total, stem_len)
    chosen = groups.reshape(row_total)
    piece = lax.all_gather(out_proj, "half", axis=0, tiled=True)
    wides = jax.vmap(widen)(piece)
    product = jnp.einsum("irk,gijkd->gjrd", rows, wides, preferred_element_type=jnp.float32)
    owners = jnp.arange(piece.shape[0], dtype=jnp.int32)
    keep = chosen[None, :] == owners[:, None]
    products = jnp.where(keep[:, None, :, None], product, 0.0)
    result = jnp.sum(products, axis=0).astype(jnp.bfloat16)
    return result.reshape(1, 1, 2, row_total, out_len)


def solution(mesh):
    small = mesh.shape["modes"] == 4 and mesh.shape["half"] == 4
    placed = (
        P(None, ("slices", "modes"), "half", None, None, None),
        P(),
        P(),
        P("half", None, None, None),
        P(("slices", "modes"), "half", None, None),
    )
    return jax.shard_map(
        gathered if small else stepped,
        mesh=mesh,
        in_specs=placed,
        out_specs=P(("slices", "modes"), "half", None, None, None),
        check_vma=False,
    )
```
